32 devices in a mesh: dp: 2 (over y), gx: 4 (over x, core), gy: 4 (over z).
Axes of the slice: x: 2, y: 2, z: 4, core: 2. Of those that a mesh axis runs over, the one named last changes fastest.
Arguments:
- hidden_pre: bfloat16 [2048, 24576], P('dp', 'gx'), may hold values from -40 to 40
- out_grad: bfloat16 [2048, 6144], P(('dp', 'gx'), 'gy'), may hold values from -40 to 40
- weight: bfloat16 [24576, 6144], P('gx', 'gy'), may hold values from -0.078125 to 0.078125
- row_second: float32 [24576], P('gx'), may hold values from 2048 to 819200
- col_second: float32 [6144], P('gy'), may hold values from 2048 to 819200
Outputs:
- hidden_grad: bfloat16 [2048, 24576], P(('dp', 'gy'), 'gx')
- update: bfloat16 [24576, 6144], P('gx', 'gy')
The draws below stay inside these ranges and needn't reach their ends.
All inputs are finite; a program needn't handle non-finite values.
Results may differ from the reference program's by a relative error of at most 0.018.
Values may be sent and summed in bfloat16 or wider, within the bound.
A program may use at most 192 MiB of HBM per device.

```python
import math
import jax
import jax.numpy as jnp
from jax import lax

D = 6144
FF = 24576
TOK_GROUP = 1024
TOKENS = 2048
N_DP = 2
N_GY = 4


def scaled_field(key, rows, cols):
    keys = jax.random.split(key, 3)
    rising = jnp.exp(math.log(3.0) * jnp.arange(cols, dtype=jnp.float32) / cols)
    col_scale = rising * jnp.exp(jax.random.uniform(keys[0], (1, cols), jnp.float32, math.log(0.4), math.log(4.0)))
    row_scale = jnp.exp(jax.random.uniform(keys[1], (rows, 1), jnp.float32, math.log(0.5), math.log(2.0)))
    base = jax.random.normal(keys[2], (rows, cols), jnp.float32)
    return jnp.clip(base * col_scale * row_scale, -40.0, 40.0)


def draw_hidden_pre(key, part):
    return scaled_field(jax.random.fold_in(key, 11), TOKENS, FF).astype(jnp.bfloat16)


def draw_out_grad(key, part):
    return scaled_field(jax.random.fold_in(key, 23), TOKENS, D).astype(jnp.bfloat16)


def level_of(stream_key, extent, pieces, smallest, high):
    factor_of, own = 1.0, jax.random.fold_in(stream_key, 6)
    for position, blocks in pieces:
        steps = jnp.exp(jax.random.uniform(jax.random.fold_in(own, position), (blocks,), jnp.float32, smallest / len(pieces), high / len(pieces)))
        factor_of = factor_of * jnp.repeat(steps, extent[position] // blocks).reshape([-1 if axis == position else 1 for axis in range(len(extent))])
    return factor_of


def gaussian(stream_key, shape, spread, most, pieces=(), kind=jnp.bfloat16):
    entries = spread * jax.random.normal(stream_key, shape, jnp.float32)
    if pieces:
        entries = entries * level_of(stream_key, shape, pieces, -0.22, 0.18)
    return jnp.clip(entries, -most, most).astype(kind)


def setup_inputs(seed: int = 0) -> dict:
    arg_keys = jax.random.split(jax.random.key(seed), 6)
    return {
        "hidden_pre": draw_hidden_pre(jax.random.fold_in(arg_keys[5], 71), 0),
        "out_grad": draw_out_grad(jax.random.fold_in(arg_keys[5], 71), 0),
        "weight": gaussian(arg_keys[2], (FF, D), D ** -0.5, 0.078125, ((0, 4), (1, 4))),
        "row_second": jnp.clip(jnp.exp(math.log(819200.0) - 5.9914645 * jax.random.uniform(arg_keys[3], (FF,), jnp.float32) ** level_of(arg_keys[3], (FF,), ((0, 4),), -0.2, 0.2)), 2048.0, 819200.0),
        "col_second": jnp.clip(jnp.exp(math.log(819200.0) - 5.9914645 * jax.random.uniform(arg_keys[4], (D,), jnp.float32) ** level_of(arg_keys[4], (D,), ((0, 4),), -0.2, 0.2)), 2048.0, 819200.0),
    }


half_root = 0.7071067811865476
inv_root_tau = 0.3989422804014327

def gelu_parts(pre_act):
    pre_act = pre_act.astype(jnp.float32)
    normal_cdf = 0.5 * (1.0 + jax.scipy.special.erf(pre_act * half_root))
    density = jnp.exp(-0.5 * pre_act * pre_act) * inv_root_tau
    return (pre_act * normal_cdf, normal_cdf + pre_act * density)

def reference(hidden_pre, out_grad, weight, row_second, col_second):
    activated_f, slopes = gelu_parts(hidden_pre)
    activated = activated_f.astype(jnp.bfloat16)
    width = D // N_GY
    grad_blocks = out_grad.reshape(TOKENS, N_GY, width).transpose(1, 0, 2)
    weight_blocks = weight.reshape(FF, N_GY, width).transpose(1, 0, 2)

    def add_block(running, blocks):
        part_prod = lax.dot_general(blocks[0], blocks[1], (((1,), (1,)), ((), ())), preferred_element_type=jnp.float32)
        rounded = lax.optimization_barrier(part_prod.astype(jnp.bfloat16))
        return (running + rounded.astype(jnp.float32), None)
    input_sum, _ = lax.scan(add_block, jnp.zeros((TOKENS, FF), jnp.float32), (grad_blocks, weight_blocks))
    hidden_grad = (input_sum * slopes).astype(jnp.bfloat16)
    act_groups = activated.reshape(N_DP, TOK_GROUP, FF)
    out_groups = out_grad.reshape(N_DP, TOK_GROUP, D)

    def add_group(running, groups):
        part_prod = lax.dot_general(groups[0], groups[1], (((0,), (0,)), ((), ())), preferred_element_type=jnp.float32)
        rounded = lax.optimization_barrier(part_prod.astype(jnp.bfloat16))
        return (running + rounded.astype(jnp.float32), None)
    grad, _ = lax.scan(add_group, jnp.zeros((FF, D), jnp.float32), (act_groups, out_groups))
    squares = grad * grad + 1e-30
    row_new = 0.5 * row_second + 0.5 * lax.optimization_barrier(jnp.mean(squares, axis=1))
    col_new = 0.5 * col_second + 0.5 * lax.optimization_barrier(jnp.mean(squares, axis=0))
    second = row_new[:, None] * col_new[None, :] / jnp.mean(row_new)
    update = (grad * lax.rsqrt(second)).astype(jnp.bfloat16)
    return (hidden_grad, update)
```

```python
import functools

import jax
import jax.numpy as jnp
from jax import lax
from jax.experimental import pallas as pl
from jax.experimental.pallas import tpu as pltpu
from jax.sharding import PartitionSpec as P

half_root = 0.7071067811865476
inv_root_tau = 0.3989422804014327
SLOTS = 4
SUBS = 4
HALVES = 2


def gelu_of(pre_act):
    pre_act = pre_act.astype(jnp.float32)
    normal_cdf = 0.5 * (1.0 + lax.erf(pre_act * half_root))
    return (pre_act * normal_cdf).astype(jnp.bfloat16)


def slopes_of(pre_act):
    pre_act = pre_act.astype(jnp.float32)
    normal_cdf = 0.5 * (1.0 + lax.erf(pre_act * half_root))
    density = jnp.exp(-0.5 * pre_act * pre_act) * inv_root_tau
    return normal_cdf + pre_act * density


def grad_kernel(n_groups, q_ref, *refs):
    acts, outs = refs[:n_groups], refs[n_groups : 2 * n_groups]
    grad_ref, row_ref, col_ref = refs[-3:]
    total = None
    for act_ref, out_ref in zip(acts, outs):
        term = jnp.dot(act_ref[...], out_ref[...], preferred_element_type=jnp.float32)
        total = term if total is None else total + term
    grad_ref[...] = total.astype(grad_ref.dtype)
    squares = total * total + 1e-30
    rows = jnp.sum(squares, axis=1, keepdims=True)
    row_ref[...] = jnp.broadcast_to(rows, (rows.shape[0], 128)).T[0:1]

    @pl.when(pl.program_id(0) == 0)
    def _():
        col_ref[...] = jnp.zeros_like(col_ref)

    col_ref[...] += jnp.sum(squares, axis=0, keepdims=True)


def grad_rows(quarter, acts, outs, buffers, hidden):
    n_groups = len(acts)
    rows, tokens = acts[0].shape
    width = outs[0].shape[1]
    block = 256 if rows % 256 == 0 else rows
    steps = rows // block
    own = pl.BlockSpec((block, tokens), lambda i, q: (i, 0))
    whole = pl.BlockSpec((tokens, width), lambda i, q: (0, 0))
    extra = [] if buffers is None else list(buffers)
    aliases = {} if buffers is None else {1 + 2 * n_groups: 0, 2 + 2 * n_groups: 1}
    return pl.pallas_call(
        functools.partial(grad_kernel, n_groups),
        grid_spec=pltpu.PrefetchScalarGridSpec(
            num_scalar_prefetch=1,
            grid=(steps,),
            in_specs=[own] * n_groups
            + [whole] * n_groups
            + [pl.BlockSpec(memory_space=pl.ANY)] * len(extra),
            out_specs=[
                pl.BlockSpec((block, width), lambda i, q: (q[0] * steps + i, 0)),
                pl.BlockSpec((1, block), lambda i, q: (0, q[0] * steps + i)),
                pl.BlockSpec((1, width), lambda i, q: (0, 0)),
            ],
        ),
        out_shape=[
            jax.ShapeDtypeStruct((hidden, width), jnp.bfloat16),
            jax.ShapeDtypeStruct((1, hidden), jnp.float32),
            jax.ShapeDtypeStruct((1, width), jnp.float32),
        ],
        input_output_aliases=aliases,
        cost_estimate=pl.CostEstimate(
            flops=2 * rows * tokens * n_groups * width,
            bytes_accessed=2 * (rows * tokens + tokens * width) * n_groups + 2 * rows * width,
            transcendentals=0,
        ),
    )(jnp.reshape(quarter, (1,)).astype(jnp.int32), *acts, *outs, *extra)


def on_device(n_dp, n_gx, n_gy, hidden_pre, out_grad, weight, row_second, col_second):
    z = lax.axis_index("gy")
    odd = lax.rem(z, 2)
    tokens, hidden = hidden_pre.shape
    width = weight.shape[1]
    part = hidden // SLOTS
    rows_here = tokens // n_gy
    model = width * n_gy
    all_hidden = hidden * n_gx

    def dp_shift(value, k):
        return lax.ppermute(value, "dp", [(i, (i + k) % n_dp) for i in range(n_dp)])

    quarters = [jnp.where(odd == 1, s, SLOTS - 1 - s) for s in range(SLOTS)]
    own_acts = [
        gelu_of(lax.dynamic_slice_in_dim(hidden_pre, q * part, part, 1)).T for q in quarters
    ]

    gathered = lax.all_gather(out_grad, "gx", axis=0, tiled=True)

    swaps = [(i, j) for a in range(1, n_gy - 1, 2) for i, j in ((a, a + 1), (a + 1, a))]
    ends = [(1, 0), (n_gy - 2, n_gy - 1)]
    at_end = (z == 0) | (z == n_gy - 1)
    sub = part // SUBS
    other_acts = [[None] * SLOTS for _ in range(n_dp)]
    for k in range(1, n_dp):
        first, relayed = [], []
        for j in range(SUBS):
            got = dp_shift(own_acts[0][j * sub : (j + 1) * sub], k)
            first.append(got)
            inner = lax.ppermute(got, "gy", swaps)
            outer = lax.ppermute(got, "gy", ends)
            relayed.append(jnp.where(at_end, outer, inner))
        other_acts[k][0] = jnp.concatenate(first, 0)
        other_acts[k][SLOTS - 1] = jnp.concatenate(relayed, 0)
    others = [None] + [
        lax.all_gather(dp_shift(out_grad, k), "gx", axis=0, tiled=True) for k in range(1, n_dp)
    ]
    for s in range(1, SLOTS - 1):
        for k in range(1, n_dp):
            other_acts[k][s] = dp_shift(own_acts[s], k)

    cut = hidden // HALVES

    def product(chunk, h):
        rows = lax.dynamic_slice_in_dim(gathered, chunk * rows_here, rows_here, 0)
        prod = lax.dot_general(
            rows, weight[h * cut : (h + 1) * cut], (((1,), (1,)), ((), ())),
            preferred_element_type=jnp.float32,
        )
        return lax.optimization_barrier(prod.astype(jnp.bfloat16))

    def plus(held, prod):
        if held is None:
            return prod
        return (held.astype(jnp.float32) + prod.astype(jnp.float32)).astype(jnp.bfloat16)

    up, down = [None] * HALVES, [None] * HALVES
    for r in range(1, n_gy):
        up_chunk = jnp.clip(z + n_gy - r, 0, n_gy - 1)
        down_chunk = jnp.clip(z - n_gy + r, 0, n_gy - 1)
        for h in range(HALVES):
            if 2 * r <= n_gy:
                prod_up = prod_down = product(jnp.where(z < r, up_chunk, down_chunk), h)
            else:
                prod_up, prod_down = product(up_chunk, h), product(down_chunk, h)
            up[h] = lax.ppermute(
                plus(up[h], prod_up), "gy", [(i, i + 1) for i in range(r)]
            )
            down[h] = lax.ppermute(
                plus(down[h], prod_down), "gy", [(n_gy - 1 - i, n_gy - 2 - i) for i in range(r)]
            )
    own_rows = lax.dynamic_slice_in_dim(hidden_pre, z * rows_here, rows_here, 0)
    pieces = []
    for h in range(HALVES):
        mine = product(z, h).astype(jnp.float32)
        summed = mine + up[h].astype(jnp.float32) + down[h].astype(jnp.float32)
        pieces.append(
            (summed * slopes_of(own_rows[:, h * cut : (h + 1) * cut])).astype(jnp.bfloat16)
        )
    hidden_grad = jnp.concatenate(pieces, 1)

    buffers, col_here = None, 0.0
    for s in [0, SLOTS - 1] + list(range(1, SLOTS - 1)):
        acts = [own_acts[s]] + [other_acts[k][s] for k in range(1, n_dp)]
        outs = [gathered] + others[1:]
        grad, row_here, col_part = grad_rows(quarters[s], acts, outs, buffers, hidden)
        buffers = (grad, row_here)
        col_here = col_here + col_part[0]
    row_total = lax.psum(row_here[0], "gy")
    row_new = 0.5 * row_second + 0.5 * row_total / model
    col_total, row_sum = lax.psum((col_here, jnp.sum(row_new)), "gx")
    col_new = 0.5 * col_second + 0.5 * col_total / all_hidden
    row_scale = lax.rsqrt(row_new)
    col_scale = lax.rsqrt(col_new) * jnp.sqrt(row_sum / all_hidden)
    update = (grad.astype(jnp.float32) * row_scale[:, None] * col_scale[None, :]).astype(jnp.bfloat16)
    return (hidden_grad, update)


def solution(mesh):
    sizes = [mesh.shape[name] for name in ("dp", "gx", "gy")]
    return jax.shard_map(
        functools.partial(on_device, *sizes),
        mesh=mesh,
        in_specs=(P("dp", "gx"), P(("dp", "gx"), "gy"), P("gx", "gy"), P("gx"), P("gy")),
        out_specs=(P(("dp", "gy"), "gx"), P("gx", "gy")),
        check_vma=False,
    )
```
